128 devices in a mesh: dp: 8 (over z_hi, x), ctx: 16 (over z_lo, y, core).
Axes of the slice: x: 4, y: 4, z: 4 (z_hi: 2, z_lo: 2; z = z_hi * 2 + z_lo), core: 2. Of those that a mesh axis runs over, the one named last changes fastest.
Arguments:
- resid: bfloat16 [16384, 4096], P(('dp', 'ctx')), may hold values from -6 to 6
- query: bfloat16 [16384, 2048], P(('dp', 'ctx')), may hold values from -40 to 40
- keys: bfloat16 [16384, 512], P(('dp', 'ctx')), may hold values from -40 to 40
- values: bfloat16 [16384, 512], P(('dp', 'ctx')), may hold values from -6 to 6
- doc_lengths: int32 [16], replicated, may hold values from 1 to 2048, 16384 in all
- w_out: bfloat16 [2048, 4096], P('dp'), may hold values from -0.125 to 0.125
- norm_gain: float32 [4096], replicated, may hold values from 0.1 to 1.9
- w_gate: bfloat16 [4096, 7168], P(None, 'dp'), may hold values from -0.09375 to 0.09375
- w_up: bfloat16 [4096, 7168], P(None, 'dp'), may hold values from -0.09375 to 0.09375
- w_down: bfloat16 [7168, 4096], P('dp'), may hold values from -0.0625 to 0.0625
Outputs:
- layer_out: bfloat16 [16384, 4096], P(('dp', 'ctx'))
The draws below stay inside these ranges and needn't reach their ends.
Inputs may be any that keep to these rules, and one draw needn't show every extreme that they name: `doc_lengths`: the lengths sum to 16384, and the longest is exactly 2048.
All inputs are finite; a program needn't handle non-finite values.
Results may differ from the reference program's by a relative error of at most 0.015.
Values may be sent and summed in bfloat16 or wider, within the bound.
A program may use at most 192 MiB of HBM per device.

```python
import math
import jax
import jax.numpy as jnp
import numpy as np
from jax import lax

D = 4096
HEADS = 16
KV_HEADS = 4
HEAD_DIM = 128
FF = 7168
TOK_DEV = 128
NDOCS = 16
SPAN = 16
TOKENS = 16384
FF_BLOCK = 896
N_DP = 8
N_CTX = 16


def key_field(key):
    return jax.random.normal(jax.random.fold_in(key, 101), (TOKENS, KV_HEADS * HEAD_DIM), jnp.float32)


def draw_keys(key, part):
    field = key_field(key)
    return jnp.clip(field, -40.0, 40.0).astype(jnp.bfloat16)


def draw_query(key, part):
    field = jax.random.normal(jax.random.fold_in(key, 202), (TOKENS, HEADS * HEAD_DIM), jnp.float32)
    return jnp.clip(field, -40.0, 40.0).astype(jnp.bfloat16)


def block_levels(stream_key, extent, pieces, smallest, largest):
    gain, own = 1.0, jax.random.fold_in(stream_key, 6)
    for axis_at, blocks in pieces:
        draws = jnp.exp(jax.random.uniform(jax.random.fold_in(own, axis_at), (blocks,), jnp.float32, smallest / len(pieces), largest / len(pieces)))
        gain = gain * jnp.repeat(draws, extent[axis_at] // blocks).reshape([-1 if axis == axis_at else 1 for axis in range(len(extent))])
    return gain


def split_up(number_of, total, limit, lean):
    loads = [(1 << 20) // math.isqrt(rank ** lean) + 1 for rank in range(2, number_of + 1)]
    surplus, holding = total - limit - (number_of - 1), [1] * (number_of - 1)
    while surplus > 0:
        free = [i for i in range(number_of - 1) if holding[i] < limit]
        pool, remaining = sum([loads[i] for i in free]), surplus
        for i in free:
            extra = min(limit - holding[i], max(1, remaining * loads[i] // pool), surplus)
            holding[i] = holding[i] + extra
            surplus = surplus - extra
    return np.array([limit] + holding)


def ragged_sizes(rng, count, total, most, slope):
    if count == 2:
        one = jax.random.randint(rng, (), max(1, total - most), min(most, total - 1) + 1)
        return jnp.stack([one, total - one])
    lengths = jnp.asarray(split_up(count, total, most, slope), jnp.int32)
    couples = (count - 1) // 2
    giver, taker = lengths[1:1 + 2 * couples:2], lengths[2:2 + 2 * couples:2]
    margin = jnp.minimum(giver - 1, most - taker)
    moved = jax.random.randint(jax.random.fold_in(rng, 1), (couples,), 0, 1 << 20) % (margin + 1)
    lengths = lengths.at[1:1 + 2 * couples:2].set(giver - moved).at[2:2 + 2 * couples:2].set(taker + moved)
    return lengths[jax.random.permutation(jax.random.fold_in(rng, 2), count)]


def noise(stream_key, dims, spread, limit, shards=(), kind=jnp.bfloat16):
    array = jax.random.normal(stream_key, dims, jnp.float32) * spread
    if len(shards) > 0:
        array = block_levels(stream_key, dims, shards, -0.22, 0.18) * array
    return jnp.clip(array, min=-limit, max=limit).astype(kind)


def setup_inputs(seed: int = 0) -> dict:
    seeds = jax.random.split(jax.random.key(seed), 11)
    resid = noise(seeds[0], (TOKENS, D), 1.0, 6.0, ((0, 128),))
    query = draw_query(jax.random.fold_in(seeds[10], 71), 0)
    keys = draw_keys(jax.random.fold_in(seeds[10], 71), 0)
    values = noise(seeds[3], (TOKENS, KV_HEADS * HEAD_DIM), 1.0, 6.0, ((0, 128),))
    doc_lengths = ragged_sizes(seeds[4], NDOCS, TOKENS, SPAN * TOK_DEV, 2).astype(jnp.int32)
    w_out = noise(seeds[5], (HEADS * HEAD_DIM, D), (HEADS * HEAD_DIM) ** -0.5, 0.125, ((0, 8),))
    norm_gain = jnp.clip(1.0 + 0.18 * jax.random.normal(seeds[6], (D,), jnp.float32), 0.1, 1.9)
    w_gate = noise(seeds[7], (D, FF), D ** -0.5, 0.09375, ((1, 8),))
    w_up = noise(seeds[8], (D, FF), D ** -0.5, 0.09375, ((1, 8),))
    w_down = noise(seeds[9], (FF, D), FF ** -0.5, 0.0625, ((0, 8),))
    return dict(resid=resid, query=query, keys=keys, values=values, doc_lengths=doc_lengths, w_out=w_out, norm_gain=norm_gain, w_gate=w_gate, w_up=w_up, w_down=w_down)


ROPE_BASE = 500000.0
EPS = 1e-05
NEG_FILL = -1e+30

def rope_tables(rel_pos, head_dim):
    half_dim = head_dim // 2
    freq_index = jnp.arange(half_dim, dtype=jnp.float32)
    inv_freq = jnp.exp(freq_index * (-2.0 * math.log(ROPE_BASE) / head_dim))
    angles = rel_pos.astype(jnp.float32)[:, None] * inv_freq[None, :]
    return (jnp.cos(angles), jnp.sin(angles))

def rotate(field, cosine, sine_val, num_heads, head_dim):
    row_count = field.shape[0]
    half_dim = head_dim // 2
    shaped = field.astype(jnp.float32).reshape(row_count, num_heads, head_dim)
    first_half = shaped[..., :half_dim]
    second_half = shaped[..., half_dim:]
    cos_b = cosine[:, None, :]
    sin_b = sine_val[:, None, :]
    turned = jnp.concatenate([first_half * cos_b - second_half * sin_b, second_half * cos_b + first_half * sin_b], axis=-1)
    return turned.reshape(row_count, num_heads * head_dim).astype(jnp.bfloat16)

def doc_starts(doc_lengths, positions):
    doc_ends = jnp.cumsum(doc_lengths).astype(jnp.int32)
    starts = (doc_ends - doc_lengths).astype(jnp.int32)
    inside = starts[None, :] <= positions[:, None]
    return lax.optimization_barrier(jnp.max(jnp.where(inside, starts[None, :], 0), axis=1)).astype(jnp.int32)

def reference(resid, query, keys, values, doc_lengths, w_out, norm_gain, w_gate, w_up, w_down):
    tok_rows = TOK_DEV
    blocks = N_DP * N_CTX
    group_size = HEADS // KV_HEADS
    positions = jnp.arange(TOKENS, dtype=jnp.int32)
    starts = doc_starts(doc_lengths, positions)
    cosine, sine_val = rope_tables(positions - starts, HEAD_DIM)
    q_rot = rotate(query, cosine, sine_val, HEADS, HEAD_DIM)
    k_rot = rotate(keys, cosine, sine_val, KV_HEADS, HEAD_DIM)
    reach_rows = SPAN * tok_rows
    keys_padded = jnp.concatenate([jnp.zeros((reach_rows, KV_HEADS * HEAD_DIM), jnp.bfloat16), k_rot], axis=0)
    values_padded = jnp.concatenate([jnp.zeros((reach_rows, KV_HEADS * HEAD_DIM), jnp.bfloat16), values], axis=0)
    score_scale = 1.0 / math.sqrt(HEAD_DIM)

    def attend(block_index):
        first_row = (block_index * tok_rows).astype(jnp.int32)
        q_block = lax.dynamic_slice_in_dim(q_rot, first_row, tok_rows, 0)
        k_block = lax.dynamic_slice_in_dim(keys_padded, first_row, reach_rows + tok_rows, 0)
        v_block = lax.dynamic_slice_in_dim(values_padded, first_row, reach_rows + tok_rows, 0)
        query_pos = first_row + jnp.arange(tok_rows, dtype=jnp.int32)
        query_start = lax.dynamic_slice_in_dim(starts, first_row, tok_rows, 0)
        key_pos = first_row - reach_rows + jnp.arange(reach_rows + tok_rows, dtype=jnp.int32)
        allowed = (key_pos[None, :] >= query_start[:, None]) & (key_pos[None, :] <= query_pos[:, None])
        q_heads = q_block.astype(jnp.float32).reshape(tok_rows, KV_HEADS, group_size, HEAD_DIM)
        key_heads = k_block.astype(jnp.float32).reshape(-1, KV_HEADS, HEAD_DIM)
        value_heads = v_block.astype(jnp.float32).reshape(-1, KV_HEADS, HEAD_DIM)
        scores = jnp.einsum('tagd,kad->agtk', q_heads, key_heads) * score_scale
        scores = jnp.where(allowed[None, None], scores, NEG_FILL)
        row_max = lax.optimization_barrier(jnp.max(scores, axis=-1, keepdims=True))
        weights = jnp.where(allowed[None, None], jnp.exp(scores - row_max), 0.0)
        row_sum = lax.optimization_barrier(jnp.sum(weights, axis=-1))
        rounded = lax.optimization_barrier(weights.astype(jnp.bfloat16)).astype(jnp.float32)
        mixed = jnp.einsum('agtk,kad->agtd', rounded, value_heads)
        heads_out = mixed / row_sum[..., None]
        return heads_out.transpose(2, 0, 1, 3).reshape(tok_rows, HEADS * HEAD_DIM).astype(jnp.bfloat16)
    attn = lax.map(attend, jnp.arange(blocks, dtype=jnp.int32)).reshape(TOKENS, HEADS * HEAD_DIM)
    residual_sum = resid.astype(jnp.float32) + jnp.dot(attn, w_out, preferred_element_type=jnp.float32)
    mean_sq = lax.optimization_barrier(jnp.mean(residual_sum * residual_sum, axis=1, keepdims=True))
    normed = (residual_sum * lax.rsqrt(mean_sq + EPS) * norm_gain).astype(jnp.bfloat16)

    def mlp_block(row_slice):
        gate_val = jnp.dot(row_slice, w_gate, preferred_element_type=jnp.float32)
        up_val = jnp.dot(row_slice, w_up, preferred_element_type=jnp.float32)
        hidden_act = (jax.nn.silu(gate_val) * up_val).astype(jnp.bfloat16)
        mlp_sum = jnp.zeros((row_slice.shape[0], D), jnp.float32)
        for ff_part in range(N_DP):
            low_col = ff_part * FF_BLOCK
            piece_sum = jnp.dot(hidden_act[:, low_col:low_col + FF_BLOCK], w_down[low_col:low_col + FF_BLOCK], preferred_element_type=jnp.float32)
            rounded = lax.optimization_barrier(piece_sum.astype(jnp.bfloat16))
            mlp_sum = mlp_sum + rounded.astype(jnp.float32)
        return mlp_sum
    mlp_out = lax.map(mlp_block, normed.reshape(blocks, tok_rows, D)).reshape(TOKENS, D)
    return (residual_sum + mlp_out).astype(jnp.bfloat16)
```

```python
import math

import jax
import jax.numpy as jnp
from jax import lax
from jax.experimental import pallas as pl
from jax.experimental.pallas import tpu as pltpu
from jax.sharding import PartitionSpec as P

HEAD_DIM = 128


ROPE_BASE = 500000.0
EPS = 1e-05
NEG_FILL = -1e30


def from_behind(block, axis, distance):
    devices = range(lax.axis_size(axis))
    route = [(i - distance, i) for i in devices if i - distance in devices]
    return lax.ppermute(block, axis, route)


def rope_tables(rel_pos, head_dim):
    half_dim = head_dim // 2
    freq_index = jnp.arange(half_dim, dtype=jnp.float32)
    inv_freq = jnp.exp(freq_index * (-2.0 * math.log(ROPE_BASE) / head_dim))
    angles = rel_pos.astype(jnp.float32)[:, None] * inv_freq[None, :]
    return (jnp.cos(angles), jnp.sin(angles))


def rotate(field, cosine, sine_val, num_heads, head_dim):
    row_count = field.shape[0]
    half_dim = head_dim // 2
    shaped = field.astype(jnp.float32).reshape(row_count, num_heads, head_dim)
    first_half = shaped[..., :half_dim]
    second_half = shaped[..., half_dim:]
    cos_b = cosine[:, None, :]
    sin_b = sine_val[:, None, :]
    turned = jnp.concatenate(
        [first_half * cos_b - second_half * sin_b, second_half * cos_b + first_half * sin_b],
        axis=-1,
    )
    return turned.reshape(row_count, num_heads * head_dim).astype(jnp.bfloat16)


def doc_starts(doc_lengths, positions):
    doc_ends = jnp.cumsum(doc_lengths)
    starts = doc_ends - doc_lengths
    inside = starts[None, :] <= positions[:, None]
    return jnp.max(jnp.where(inside, starts[None, :], 0), axis=1)


def online_update(
    softmax_state, q_group, key_rows, value_rows, key_pos, query_pos, query_start, score_scale
):
    row_max, row_sum, weighted = softmax_state
    kv_heads = q_group.shape[0]
    head_dim = q_group.shape[2]
    key_heads = key_rows.reshape(key_rows.shape[0], kv_heads, head_dim).transpose(1, 0, 2)
    value_heads = value_rows.reshape(value_rows.shape[0], kv_heads, head_dim).transpose(1, 0, 2)
    scores = (
        jnp.einsum("aqd,akd->aqk", q_group, key_heads, preferred_element_type=jnp.float32)
        * score_scale
    )
    allowed = (key_pos[None, :] >= query_start[:, None]) & (key_pos[None, :] <= query_pos[:, None])
    group_size = q_group.shape[1] // query_pos.shape[0]
    allowed = jnp.tile(allowed, (group_size, 1))[None]
    scores = jnp.where(allowed, scores, NEG_FILL)
    new_max = jnp.maximum(row_max, jnp.max(scores, axis=-1))
    weights = jnp.where(allowed, jnp.exp(scores - new_max[..., None]), 0.0)
    factor = jnp.exp(row_max - new_max)
    row_sum = row_sum * factor + jnp.sum(weights, axis=-1)
    weighted = weighted * factor[..., None] + jnp.einsum(
        "aqk,akd->aqd",
        weights.astype(jnp.bfloat16),
        value_heads,
        preferred_element_type=jnp.float32,
    )
    return (new_max, row_sum, weighted)


MESH = pl.DeviceIdType.MESH


def dp_neighbours():
    dp_at = lax.axis_index("dp")
    ctx_at = lax.axis_index("ctx")
    ring = (dp_at // 4) * 4
    x_at = dp_at % 4
    right = (ring + (x_at + 1) % 4, ctx_at)
    left = (ring + (x_at + 3) % 4, ctx_at)
    across = ((dp_at + 4) % 8, ctx_at)
    return right, left, across


BLOCKS = ((0, 0), (1, 0), (0, 1), (0, 3), (0, 2), (1, 1), (1, 2), (1, 3))
SLOT = {name: at for at, name in enumerate(BLOCKS)}


def mlp_kernel(
    normed_ref, resid_ref, gate_hbm, up_hbm, down_hbm, out_ref,
    tokens, gate_w, up_w, down_w, hidden, sums,
    far_1, far_2, near_1, near_2, cross_1, cross_2,
    local_sem, send_sem, recv_sem,
):
    right, left, across = dp_neighbours()
    rows = tokens.shape[1]
    q = rows // 4
    low, high = pl.ds(0, 2 * q), pl.ds(2 * q, 2 * q)
    part = [pl.ds(i * q, q) for i in range(4)]

    own = pltpu.make_async_copy(normed_ref, tokens.at[0], local_sem.at[0])
    own.start()
    loads = [
        pltpu.make_async_copy(gate_hbm, gate_w, local_sem.at[1]),
        pltpu.make_async_copy(up_hbm, up_w, local_sem.at[2]),
        pltpu.make_async_copy(down_hbm, down_w, local_sem.at[3]),
    ]

    barrier = pltpu.get_barrier_semaphore()
    for peer in (right, left, across):
        pl.semaphore_signal(barrier, inc=1, device_id=peer, device_id_type=MESH)
    pl.semaphore_wait(barrier, 3)

    def slot(dz, dx):
        return SLOT[(dz, dx)]

    plan = {}

    def add(name, src, dst, peer):
        plan[name] = (src, dst, peer, len(plan))

    def copy(name):
        src, dst, peer, at = plan[name]
        return pltpu.make_async_remote_copy(
            src_ref=src, dst_ref=dst, send_sem=send_sem.at[at], recv_sem=recv_sem.at[at],
            device_id=peer, device_id_type=MESH,
        )

    def tok(dz, dx, sel):
        return tokens.at[slot(dz, dx), sel]

    def res(dz, dx, sel):
        return sums.at[slot(dz, dx), sel]

    for i in range(4):
        add(("r", 0, i), tok(0, 0, part[i]), tok(0, 3, part[i]), right)
        add(("l", 0, i), tok(0, 0, part[i]), tok(0, 1, part[i]), left)
    for i in range(2):
        add(("r", 1, i), tok(1, 0, part[i]), tok(1, 3, part[i]), right)
        add(("l", 1, i), tok(1, 0, part[i]), tok(1, 1, part[i]), left)
    for dz, i in ((0, 0), (0, 2), (1, 0)):
        add(("rr", dz, i), tok(dz, 3, part[i]), tok(dz, 2, part[i]), right)
        add(("ll", dz, i + 1), tok(dz, 1, part[i + 1]), tok(dz, 2, part[i + 1]), left)
    add(("z", 0, 0), tok(0, 0, low), tok(1, 0, low), across)
    for dx in range(4):
        add(("z", dx, 1), tok(0, dx, high), tok(1, dx, high), across)
    for dz in range(2):
        add(("fr", dz), res(dz, 2, part[0]), far_1.at[dz, 0], right)
        add(("fl", dz), res(dz, 2, part[1]), far_1.at[dz, 1], left)
        add(("nr", dz), res(dz, 1, low), near_1.at[dz, 0], right)
        add(("nl", dz), res(dz, 3, low), near_1.at[dz, 1], left)
    add("fr2", res(0, 2, part[2]), far_2.at[0], right)
    add("fl2", res(0, 2, part[3]), far_2.at[1], left)
    add("nr2", res(0, 1, high), near_2.at[0], right)
    add("nl2", res(0, 3, high), near_2.at[1], left)
    for dx in range(4):
        add(("sz", dx), res(1, dx, high), cross_2.at[dx], across)
    add("sz1", res(1, 0, low), cross_1, across)

    def start(*names):
        for name in names:
            copy(name).start()

    def arrived(*names):
        for name in names:
            copy(name).wait_recv()

    def grow(dz, dx, sel, *terms):
        ref = res(dz, dx, sel)
        total = ref[...].astype(jnp.float32)
        for term in terms:
            total = total + term[...].astype(jnp.float32)
        ref[...] = total.astype(jnp.bfloat16)

    own.wait()
    start(("z", 0, 0), ("r", 0, 2), ("l", 0, 3), ("r", 0, 3), ("l", 0, 2), ("z", 0, 1))
    start(("r", 0, 0), ("l", 0, 1), ("r", 0, 1), ("l", 0, 0))
    for load in loads:
        load.start()

    def step(at, carry):
        @pl.when(at == 0)
        def _():
            for load in loads:
                load.wait()

        @pl.when(at == 1)
        def _():
            arrived(("r", 0, 2))
            start(("rr", 0, 2))
            arrived(("l", 0, 3))
            start(("ll", 0, 3))
            arrived(("l", 0, 2))
            start(("z", 1, 1))
            arrived(("r", 0, 0))
            start(("rr", 0, 0))
            arrived(("l", 0, 1))
            start(("ll", 0, 1))
            arrived(("z", 0, 0))
            start(("r", 1, 0), ("l", 1, 1), ("r", 1, 1), ("l", 1, 0))
            arrived(("z", 0, 1))

        @pl.when(at == 2)
        def _():
            arrived(("rr", 0, 2), ("ll", 0, 3))
            start(("z", 2, 1))
            arrived(("r", 0, 3))
            start(("z", 3, 1))
            arrived(("l", 0, 0))

        @pl.when(at == 3)
        def _():
            arrived(("r", 0, 1))

        @pl.when(at == 4)
        def _():
            arrived(("r", 1, 0))
            start(("rr", 1, 0))
            arrived(("l", 1, 1))
            start(("ll", 1, 1))
            arrived(("rr", 0, 0), ("ll", 0, 1))

        @pl.when(at == 5)
        def _():
            arrived(("l", 1, 0), ("z", 1, 1))

        @pl.when(at == 6)
        def _():
            arrived(("rr", 1, 0), ("ll", 1, 1), ("z", 2, 1))

        @pl.when(at == 7)
        def _():
            arrived(("r", 1, 1), ("z", 3, 1))

        block = tokens[at]
        width = gate_w.shape[1]
        for col in range(0, width, 256):
            cols = slice(col, min(col + 256, width))
            gate_val = jnp.dot(block, gate_w[:, cols], preferred_element_type=jnp.float32)
            up_val = jnp.dot(block, up_w[:, cols], preferred_element_type=jnp.float32)
            act = gate_val / (1.0 + jnp.exp(-gate_val)) * up_val
            hidden[:, cols] = act.astype(jnp.bfloat16)
        held = hidden[...]
        for col in range(0, down_w.shape[1], 512):
            cols = slice(col, col + 512)
            piece = jnp.dot(held, down_w[:, cols], preferred_element_type=jnp.float32)
            sums[at, :, cols] = piece.astype(jnp.bfloat16)

        @pl.when(at == 4)
        def _():
            start(("fr", 0), ("fl", 0))

        @pl.when(at == 6)
        def _():
            start(("fr", 1), ("fl", 1), ("sz", 2), ("sz", 1))

        @pl.when(at == 7)
        def _():
            start(("sz", 3), ("sz", 0))

        return carry

    lax.fori_loop(0, 8, step, 0)

    for dz in range(2):
        arrived(("fr", dz))
        grow(dz, 1, part[0], far_1.at[dz, 0])
        start(("nr", dz))
        arrived(("fl", dz))
        grow(dz, 3, part[1], far_1.at[dz, 1])
        start(("nl", dz))
    arrived(("sz", 2))
    grow(0, 2, high, cross_2.at[2])
    start("fr2", "fl2")
    arrived(("sz", 1))
    grow(0, 1, high, cross_2.at[1])
    arrived(("nr", 0), ("nl", 0))
    grow(0, 0, low, near_1.at[0, 0], near_1.at[0, 1])
    arrived(("nr", 1), ("nl", 1))
    grow(1, 0, low, near_1.at[1, 0], near_1.at[1, 1])
    start("sz1")
    arrived("fr2")
    grow(0, 1, part[2], far_2.at[0])
    start("nr2")
    arrived(("sz", 3), "fl2")
    grow(0, 3, high, cross_2.at[3])
    grow(0, 3, part[3], far_2.at[1])
    start("nl2")

    def finish(sel, *terms):
        total = res(0, 0, sel)[...].astype(jnp.float32)
        for term in terms:
            total = total + term[...].astype(jnp.float32)
        out_ref[sel, :] = (resid_ref[sel, :] + total).astype(jnp.bfloat16)

    arrived(("sz", 0), "nr2", "nl2")
    finish(high, cross_2.at[0], near_2.at[0], near_2.at[1])
    arrived("sz1")
    finish(low, cross_1)
    for name in plan:
        copy(name).wait_send()


def mlp_phase(normed, residual_sum, w_gate, w_up, w_down):
    rows, width = normed.shape
    half, quarter = rows // 2, rows // 4
    ff = w_gate.shape[1]
    anywhere = pl.BlockSpec(memory_space=pl.ANY)
    vmem = pl.BlockSpec(memory_space=pltpu.VMEM)
    bf16 = jnp.bfloat16
    copies = 8 + 4 + 6 + 5 + 8 + 4 + 5
    return pl.pallas_call(
        mlp_kernel,
        out_shape=jax.ShapeDtypeStruct((rows, width), bf16),
        in_specs=[anywhere, vmem, anywhere, anywhere, anywhere],
        out_specs=vmem,
        scratch_shapes=[
            pltpu.VMEM((8, rows, width), bf16),
            pltpu.VMEM((width, ff), bf16),
            pltpu.VMEM((width, ff), bf16),
            pltpu.VMEM((ff, width), bf16),
            pltpu.VMEM((rows, ff), bf16),
            pltpu.VMEM((8, rows, width), bf16),
            pltpu.VMEM((2, 2, quarter, width), bf16),
            pltpu.VMEM((2, quarter, width), bf16),
            pltpu.VMEM((2, 2, half, width), bf16),
            pltpu.VMEM((2, half, width), bf16),
            pltpu.VMEM((half, width), bf16),
            pltpu.VMEM((4, half, width), bf16),
            pltpu.SemaphoreType.DMA((4,)),
            pltpu.SemaphoreType.DMA((copies,)),
            pltpu.SemaphoreType.DMA((copies,)),
        ],
        compiler_params=pltpu.CompilerParams(
            collective_id=1, has_side_effects=True, vmem_limit_bytes=67043328
        ),
        name="mlp_exchange",
    )(normed, residual_sum, w_gate, w_up, w_down)


def per_device(resid, query, keys, values, doc_lengths, w_out, norm_gain, w_gate, w_up, w_down):
    tok_rows = resid.shape[0]
    dp_count = lax.axis_size("dp")
    ctx_count = lax.axis_size("ctx")
    reach_devs = min(16, dp_count * ctx_count // 4)
    head_dim = HEAD_DIM
    kv_heads = keys.shape[1] // head_dim
    num_heads = query.shape[1] // head_dim
    group_size = num_heads // kv_heads
    my_block = lax.axis_index(("dp", "ctx"))
    local_index = jnp.arange(tok_rows, dtype=jnp.int32)
    query_pos = my_block * tok_rows + local_index
    query_start = doc_starts(doc_lengths, query_pos)
    cosine, sine_val = rope_tables(query_pos - query_start, head_dim)
    q_rot = rotate(query, cosine, sine_val, num_heads, head_dim)
    k_rot = rotate(keys, cosine, sine_val, kv_heads, head_dim)
    q_group = (
        q_rot.reshape(tok_rows, kv_heads, group_size, head_dim)
        .transpose(1, 2, 0, 3)
        .reshape(kv_heads, group_size * tok_rows, head_dim)
    )
    score_scale = 1.0 / math.sqrt(head_dim)
    softmax_state = (
        jnp.full((kv_heads, group_size * tok_rows), NEG_FILL, jnp.float32),
        jnp.zeros((kv_heads, group_size * tok_rows), jnp.float32),
        jnp.zeros((kv_heads, group_size * tok_rows, head_dim), jnp.float32),
    )
    kv_pair = jnp.stack([k_rot, values])
    softmax_state = online_update(
        softmax_state, q_group, k_rot, values, query_pos, query_pos, query_start, score_scale
    )

    def cycle_free_step(turn_index, loop_state):
        inner_state, moving = loop_state
        moving = from_behind(moving, ("dp", "ctx"), 1)
        source = my_block - turn_index - 1
        inner_state = online_update(
            inner_state,
            q_group,
            moving[0],
            moving[1],
            source * tok_rows + local_index,
            query_pos,
            query_start,
            score_scale,
        )
        return (inner_state, moving)

    softmax_state, _ = lax.fori_loop(0, reach_devs, cycle_free_step, (softmax_state, kv_pair))
    row_max, row_sum, weighted = softmax_state
    heads_out = (weighted / row_sum[..., None]).reshape(kv_heads, group_size, tok_rows, head_dim)
    heads_out = (
        heads_out.transpose(2, 0, 1, 3).reshape(tok_rows, num_heads * head_dim).astype(jnp.bfloat16)
    )
    spread = lax.all_to_all(heads_out, "dp", split_axis=1, concat_axis=0, tiled=True)
    projected = lax.psum_scatter(
        jnp.dot(spread, w_out, preferred_element_type=jnp.float32).astype(jnp.bfloat16),
        "dp",
        scatter_dimension=0,
        tiled=True,
    ).astype(jnp.float32)
    residual_sum = resid.astype(jnp.float32) + projected
    mean_sq = jnp.mean(residual_sum * residual_sum, axis=1, keepdims=True)
    normed = (residual_sum * lax.rsqrt(mean_sq + EPS) * norm_gain).astype(jnp.bfloat16)
    return mlp_phase(normed, residual_sum, w_gate, w_up, w_down)


def solution(mesh):
    return jax.shard_map(
        per_device,
        mesh=mesh,
        in_specs=(
            P(("dp", "ctx"), None),
            P(("dp", "ctx"), None),
            P(("dp", "ctx"), None),
            P(("dp", "ctx"), None),
            P(),
            P("dp", None),
            P(),
            P(None, "dp"),
            P(None, "dp"),
            P("dp", None),
        ),
        out_specs=P(("dp", "ctx"), None),
        check_vma=False,
    )
```

```python
import math

import jax
import jax.numpy as jnp
from jax import lax
from jax.experimental import pallas as pl
from jax.experimental.pallas import tpu as pltpu
from jax.sharding import PartitionSpec as P

HEAD_DIM = 128


ROPE_BASE = 500000.0
EPS = 1e-05
NEG_FILL = -1e30


def rope_tables(rel_pos, head_dim):
    half_dim = head_dim // 2
    freq_index = jnp.arange(half_dim, dtype=jnp.float32)
    inv_freq = jnp.exp(freq_index * (-2.0 * math.log(ROPE_BASE) / head_dim))
    angles = rel_pos.astype(jnp.float32)[:, None] * inv_freq[None, :]
    return (jnp.cos(angles), jnp.sin(angles))


def rotate(field, cosine, sine_val, num_heads, head_dim):
    row_count = field.shape[0]
    half_dim = head_dim // 2
    shaped = field.astype(jnp.float32).reshape(row_count, num_heads, head_dim)
    first_half = shaped[..., :half_dim]
    second_half = shaped[..., half_dim:]
    cos_b = cosine[:, None, :]
    sin_b = sine_val[:, None, :]
    turned = jnp.concatenate(
        [first_half * cos_b - second_half * sin_b, second_half * cos_b + first_half * sin_b],
        axis=-1,
    )
    return turned.reshape(row_count, num_heads * head_dim).astype(jnp.bfloat16)


def doc_starts(doc_lengths, positions):
    doc_ends = jnp.cumsum(doc_lengths)
    starts = doc_ends - doc_lengths
    inside = starts[None, :] <= positions[:, None]
    return jnp.max(jnp.where(inside, starts[None, :], 0), axis=1)


MESH = pl.DeviceIdType.MESH


def dp_neighbours():
    dp_at = lax.axis_index("dp")
    ctx_at = lax.axis_index("ctx")
    ring = (dp_at // 4) * 4
    x_at = dp_at % 4
    right = (ring + (x_at + 1) % 4, ctx_at)
    left = (ring + (x_at + 3) % 4, ctx_at)
    across = ((dp_at + 4) % 8, ctx_at)
    return right, left, across


BLOCKS = ((0, 0), (1, 0), (0, 1), (0, 3), (0, 2), (1, 1), (1, 2), (1, 3))
SLOT = {name: at for at, name in enumerate(BLOCKS)}


def mlp_kernel(
    normed_ref, resid_ref, gate_hbm, up_hbm, down_hbm, out_ref,
    tokens, gate_w, up_w, down_w, hidden, sums,
    far_1, far_2, near_1, near_2, cross_1, cross_2,
    local_sem, send_sem, recv_sem,
):
    right, left, across = dp_neighbours()
    rows = tokens.shape[1]
    q = rows // 4
    low, high = pl.ds(0, 2 * q), pl.ds(2 * q, 2 * q)
    part = [pl.ds(i * q, q) for i in range(4)]

    own = pltpu.make_async_copy(normed_ref, tokens.at[0], local_sem.at[0])
    own.start()
    loads = [
        pltpu.make_async_copy(gate_hbm, gate_w, local_sem.at[1]),
        pltpu.make_async_copy(up_hbm, up_w, local_sem.at[2]),
        pltpu.make_async_copy(down_hbm, down_w, local_sem.at[3]),
    ]

    barrier = pltpu.get_barrier_semaphore()
    for peer in (right, left, across):
        pl.semaphore_signal(barrier, inc=1, device_id=peer, device_id_type=MESH)
    pl.semaphore_wait(barrier, 3)

    def slot(dz, dx):
        return SLOT[(dz, dx)]

    plan = {}

    def add(name, src, dst, peer):
        plan[name] = (src, dst, peer, len(plan))

    def copy(name):
        src, dst, peer, at = plan[name]
        return pltpu.make_async_remote_copy(
            src_ref=src, dst_ref=dst, send_sem=send_sem.at[at], recv_sem=recv_sem.at[at],
            device_id=peer, device_id_type=MESH,
        )

    def tok(dz, dx, sel):
        return tokens.at[slot(dz, dx), sel]

    def res(dz, dx, sel):
        return sums.at[slot(dz, dx), sel]

    for i in range(4):
        add(("r", 0, i), tok(0, 0, part[i]), tok(0, 3, part[i]), right)
        add(("l", 0, i), tok(0, 0, part[i]), tok(0, 1, part[i]), left)
    for i in range(2):
        add(("r", 1, i), tok(1, 0, part[i]), tok(1, 3, part[i]), right)
        add(("l", 1, i), tok(1, 0, part[i]), tok(1, 1, part[i]), left)
    for dz, i in ((0, 0), (0, 2), (1, 0)):
        add(("rr", dz, i), tok(dz, 3, part[i]), tok(dz, 2, part[i]), right)
        add(("ll", dz, i + 1), tok(dz, 1, part[i + 1]), tok(dz, 2, part[i + 1]), left)
    add(("z", 0, 0), tok(0, 0, low), tok(1, 0, low), across)
    for dx in range(4):
        add(("z", dx, 1), tok(0, dx, high), tok(1, dx, high), across)
    for dz in range(2):
        add(("fr", dz), res(dz, 2, part[0]), far_1.at[dz, 0], right)
        add(("fl", dz), res(dz, 2, part[1]), far_1.at[dz, 1], left)
        add(("nr", dz), res(dz, 1, low), near_1.at[dz, 0], right)
        add(("nl", dz), res(dz, 3, low), near_1.at[dz, 1], left)
    add("fr2", res(0, 2, part[2]), far_2.at[0], right)
    add("fl2", res(0, 2, part[3]), far_2.at[1], left)
    add("nr2", res(0, 1, high), near_2.at[0], right)
    add("nl2", res(0, 3, high), near_2.at[1], left)
    for dx in range(4):
        add(("sz", dx), res(1, dx, high), cross_2.at[dx], across)
    add("sz1", res(1, 0, low), cross_1, across)

    def start(*names):
        for name in names:
            copy(name).start()

    def arrived(*names):
        for name in names:
            copy(name).wait_recv()

    def grow(dz, dx, sel, *terms):
        ref = res(dz, dx, sel)
        total = ref[...].astype(jnp.float32)
        for term in terms:
            total = total + term[...].astype(jnp.float32)
        ref[...] = total.astype(jnp.bfloat16)

    own.wait()
    start(("z", 0, 0), ("r", 0, 2), ("l", 0, 3), ("r", 0, 3), ("l", 0, 2), ("z", 0, 1))
    start(("r", 0, 0), ("l", 0, 1), ("r", 0, 1), ("l", 0, 0))
    for load in loads:
        load.start()

    def step(at, carry):
        @pl.when(at == 0)
        def _():
            for load in loads:
                load.wait()

        @pl.when(at == 1)
        def _():
            arrived(("r", 0, 2))
            start(("rr", 0, 2))
            arrived(("l", 0, 3))
            start(("ll", 0, 3))
            arrived(("l", 0, 2))
            start(("z", 1, 1))
            arrived(("r", 0, 0))
            start(("rr", 0, 0))
            arrived(("l", 0, 1))
            start(("ll", 0, 1))
            arrived(("z", 0, 0))
            start(("r", 1, 0), ("l", 1, 1), ("r", 1, 1), ("l", 1, 0))
            arrived(("z", 0, 1))

        @pl.when(at == 2)
        def _():
            arrived(("rr", 0, 2), ("ll", 0, 3))
            start(("z", 2, 1))
            arrived(("r", 0, 3))
            start(("z", 3, 1))
            arrived(("l", 0, 0))

        @pl.when(at == 3)
        def _():
            arrived(("r", 0, 1))

        @pl.when(at == 4)
        def _():
            arrived(("r", 1, 0))
            start(("rr", 1, 0))
            arrived(("l", 1, 1))
            start(("ll", 1, 1))
            arrived(("rr", 0, 0), ("ll", 0, 1))

        @pl.when(at == 5)
        def _():
            arrived(("l", 1, 0), ("z", 1, 1))

        @pl.when(at == 6)
        def _():
            arrived(("rr", 1, 0), ("ll", 1, 1), ("z", 2, 1))

        @pl.when(at == 7)
        def _():
            arrived(("r", 1, 1), ("z", 3, 1))

        block = tokens[at]
        width = gate_w.shape[1]
        for col in range(0, width, 256):
            cols = slice(col, min(col + 256, width))
            gate_val = jnp.dot(block, gate_w[:, cols], preferred_element_type=jnp.float32)
            up_val = jnp.dot(block, up_w[:, cols], preferred_element_type=jnp.float32)
            act = gate_val / (1.0 + jnp.exp(-gate_val)) * up_val
            hidden[:, cols] = act.astype(jnp.bfloat16)
        held = hidden[...]
        for col in range(0, down_w.shape[1], 512):
            cols = slice(col, col + 512)
            piece = jnp.dot(held, down_w[:, cols], preferred_element_type=jnp.float32)
            sums[at, :, cols] = piece.astype(jnp.bfloat16)

        @pl.when(at == 4)
        def _():
            start(("fr", 0), ("fl", 0))

        @pl.when(at == 6)
        def _():
            start(("fr", 1), ("fl", 1), ("sz", 2), ("sz", 1))

        @pl.when(at == 7)
        def _():
            start(("sz", 3), ("sz", 0))

        return carry

    lax.fori_loop(0, 8, step, 0)

    for dz in range(2):
        arrived(("fr", dz))
        grow(dz, 1, part[0], far_1.at[dz, 0])
        start(("nr", dz))
        arrived(("fl", dz))
        grow(dz, 3, part[1], far_1.at[dz, 1])
        start(("nl", dz))
    arrived(("sz", 2))
    grow(0, 2, high, cross_2.at[2])
    start("fr2", "fl2")
    arrived(("sz", 1))
    grow(0, 1, high, cross_2.at[1])
    arrived(("nr", 0), ("nl", 0))
    grow(0, 0, low, near_1.at[0, 0], near_1.at[0, 1])
    arrived(("nr", 1), ("nl", 1))
    grow(1, 0, low, near_1.at[1, 0], near_1.at[1, 1])
    start("sz1")
    arrived("fr2")
    grow(0, 1, part[2], far_2.at[0])
    start("nr2")
    arrived(("sz", 3), "fl2")
    grow(0, 3, high, cross_2.at[3])
    grow(0, 3, part[3], far_2.at[1])
    start("nl2")

    def finish(sel, *terms):
        total = res(0, 0, sel)[...].astype(jnp.float32)
        for term in terms:
            total = total + term[...].astype(jnp.float32)
        out_ref[sel, :] = (resid_ref[sel, :] + total).astype(jnp.bfloat16)

    arrived(("sz", 0), "nr2", "nl2")
    finish(high, cross_2.at[0], near_2.at[0], near_2.at[1])
    arrived("sz1")
    finish(low, cross_1)
    for name in plan:
        copy(name).wait_send()


def mlp_phase(normed, residual_sum, w_gate, w_up, w_down):
    rows, width = normed.shape
    half, quarter = rows // 2, rows // 4
    ff = w_gate.shape[1]
    anywhere = pl.BlockSpec(memory_space=pl.ANY)
    vmem = pl.BlockSpec(memory_space=pltpu.VMEM)
    bf16 = jnp.bfloat16
    copies = 8 + 4 + 6 + 5 + 8 + 4 + 5
    return pl.pallas_call(
        mlp_kernel,
        out_shape=jax.ShapeDtypeStruct((rows, width), bf16),
        in_specs=[anywhere, vmem, anywhere, anywhere, anywhere],
        out_specs=vmem,
        scratch_shapes=[
            pltpu.VMEM((8, rows, width), bf16),
            pltpu.VMEM((width, ff), bf16),
            pltpu.VMEM((width, ff), bf16),
            pltpu.VMEM((ff, width), bf16),
            pltpu.VMEM((rows, ff), bf16),
            pltpu.VMEM((8, rows, width), bf16),
            pltpu.VMEM((2, 2, quarter, width), bf16),
            pltpu.VMEM((2, quarter, width), bf16),
            pltpu.VMEM((2, 2, half, width), bf16),
            pltpu.VMEM((2, half, width), bf16),
            pltpu.VMEM((half, width), bf16),
            pltpu.VMEM((4, half, width), bf16),
            pltpu.SemaphoreType.DMA((4,)),
            pltpu.SemaphoreType.DMA((copies,)),
            pltpu.SemaphoreType.DMA((copies,)),
        ],
        compiler_params=pltpu.CompilerParams(
            collective_id=1, has_side_effects=True, vmem_limit_bytes=67043328
        ),
        name="mlp_exchange",
    )(normed, residual_sum, w_gate, w_up, w_down)


REACH = 16


def attention_kernel(
    q_ref, k_ref, v_ref, start_ref, out_ref,
    slots, q_rows, row_max, sums, weighted, send_sem, recv_sem,
):
    ctx_count = lax.axis_size("ctx")
    total = lax.axis_size("dp") * ctx_count
    me = lax.axis_index("dp") * ctx_count + lax.axis_index("ctx")
    ahead = (me + 1) % total
    behind = (me + total - 1) % total
    rows = k_ref.shape[0]
    kv_heads, group_rows, head_dim = q_rows.shape
    group = group_rows // rows
    scale = 1.0 / math.sqrt(head_dim)
    barrier = pltpu.get_barrier_semaphore()
    pl.semaphore_signal(
        barrier, inc=1, device_id=(behind // ctx_count, behind % ctx_count), device_id_type=MESH
    )
    slots[0, 0] = k_ref[...]
    slots[0, 1] = v_ref[...]
    received = jnp.minimum(me, REACH)
    sent = jnp.where(me == total - 1, 0, jnp.minimum(me + 1, REACH))

    def onward(t):
        return pltpu.make_async_remote_copy(
            src_ref=slots.at[t], dst_ref=slots.at[t + 1],
            send_sem=send_sem.at[t], recv_sem=recv_sem.at[t],
            device_id=(ahead // ctx_count, ahead % ctx_count), device_id_type=MESH,
        )

    pl.semaphore_wait(barrier, 1)

    @pl.when(sent > 0)
    def _():
        onward(0).start()

    for h in range(kv_heads):
        for g in range(group):
            at = (h * group + g) * head_dim
            q_rows[h, g * rows:(g + 1) * rows, :] = q_ref[:, at:at + head_dim]
    row_max[...] = jnp.full(row_max.shape, NEG_FILL, jnp.float32)
    sums[...] = jnp.zeros(sums.shape, jnp.float32)
    weighted[...] = jnp.zeros(weighted.shape, jnp.float32)

    def step(t, carry):
        @pl.when(t > 0)
        def _():
            onward(t - 1).wait_recv()

        @pl.when((t > 0) & (t < sent))
        def _():
            onward(t).start()

        key_at = (me - t) * rows + lax.broadcasted_iota(jnp.int32, (rows, rows), 1)
        query_at = me * rows + lax.broadcasted_iota(jnp.int32, (rows, rows), 0)
        allowed = (key_at >= start_ref[...]) & (key_at <= query_at)
        for h in range(kv_heads):
            cols = slice(h * head_dim, (h + 1) * head_dim)
            scores = lax.dot_general(
                q_rows[h], slots[t, 0, :, cols], (((1,), (1,)), ((), ())),
                preferred_element_type=jnp.float32,
            )
            scores = jnp.where(
                allowed[None], (scores * scale).reshape(group, rows, rows), NEG_FILL
            ).reshape(group_rows, rows)
            old_max = row_max[h]
            new_max = jnp.maximum(old_max, jnp.max(scores, axis=-1, keepdims=True))
            weights = jnp.exp(scores - new_max)
            factor = jnp.exp(old_max - new_max)
            row_max[h] = new_max
            sums[h] = sums[h] * factor + weights
            weighted[h] = weighted[h] * factor + jnp.dot(
                weights.astype(jnp.bfloat16), slots[t, 1, :, cols],
                preferred_element_type=jnp.float32,
            )
        return carry

    lax.fori_loop(0, received + 1, step, 0)
    for h in range(kv_heads):
        head_rows = weighted[h] / jnp.sum(sums[h], axis=-1, keepdims=True)
        for g in range(group):
            at = (h * group + g) * head_dim
            out_ref[:, at:at + head_dim] = head_rows[g * rows:(g + 1) * rows].astype(jnp.bfloat16)

    def drain(t, carry):
        onward(t).wait_send()
        return carry

    lax.fori_loop(0, sent, drain, 0)


def attention_phase(q_rot, k_rot, values, query_start):
    rows, width = q_rot.shape
    kv_width = k_rot.shape[1]
    kv_heads = kv_width // HEAD_DIM
    group_rows = width // kv_width * rows
    vmem = pl.BlockSpec(memory_space=pltpu.VMEM)
    per_row = (kv_heads, group_rows, HEAD_DIM)
    starts = jnp.broadcast_to(query_start[:, None], (rows, rows))
    return pl.pallas_call(
        attention_kernel,
        out_shape=jax.ShapeDtypeStruct((rows, width), jnp.bfloat16),
        in_specs=[vmem, vmem, vmem, vmem],
        out_specs=vmem,
        scratch_shapes=[
            pltpu.VMEM((REACH + 1, 2, rows, kv_width), jnp.bfloat16),
            pltpu.VMEM(per_row, jnp.bfloat16),
            pltpu.VMEM(per_row, jnp.float32),
            pltpu.VMEM(per_row, jnp.float32),
            pltpu.VMEM(per_row, jnp.float32),
            pltpu.SemaphoreType.DMA((REACH,)),
            pltpu.SemaphoreType.DMA((REACH,)),
        ],
        compiler_params=pltpu.CompilerParams(
            collective_id=2, has_side_effects=True, vmem_limit_bytes=33554432
        ),
        name="attention_chain",
    )(q_rot, k_rot, values, starts)


def per_device(resid, query, keys, values, doc_lengths, w_out, norm_gain, w_gate, w_up, w_down):
    tok_rows = resid.shape[0]
    head_dim = HEAD_DIM
    kv_heads = keys.shape[1] // head_dim
    num_heads = query.shape[1] // head_dim
    my_block = lax.axis_index(("dp", "ctx"))
    local_index = jnp.arange(tok_rows, dtype=jnp.int32)
    query_pos = my_block * tok_rows + local_index
    query_start = doc_starts(doc_lengths, query_pos)
    cosine, sine_val = rope_tables(query_pos - query_start, head_dim)
    q_rot = rotate(query, cosine, sine_val, num_heads, head_dim)
    k_rot = rotate(keys, cosine, sine_val, kv_heads, head_dim)
    heads_out = attention_phase(q_rot, k_rot, values, query_start)
    spread = lax.all_to_all(heads_out, "dp", split_axis=1, concat_axis=0, tiled=True)
    projected = lax.psum_scatter(
        jnp.dot(spread, w_out, preferred_element_type=jnp.float32).astype(jnp.bfloat16),
        "dp",
        scatter_dimension=0,
        tiled=True,
    ).astype(jnp.float32)
    residual_sum = resid.astype(jnp.float32) + projected
    mean_sq = jnp.mean(residual_sum * residual_sum, axis=1, keepdims=True)
    normed = (residual_sum * lax.rsqrt(mean_sq + EPS) * norm_gain).astype(jnp.bfloat16)
    return mlp_phase(normed, residual_sum, w_gate, w_up, w_down)


def solution(mesh):
    return jax.shard_map(
        per_device,
        mesh=mesh,
        in_specs=(
            P(("dp", "ctx"), None),
            P(("dp", "ctx"), None),
            P(("dp", "ctx"), None),
            P(("dp", "ctx"), None),
            P(),
            P("dp", None),
            P(),
            P(None, "dp"),
            P(None, "dp"),
            P("dp", None),
        ),
        out_specs=P(("dp", "ctx"), None),
        check_vma=False,
    )
```

```python
import math

import jax
import jax.numpy as jnp
from jax import lax
from jax.experimental import pallas as pl
from jax.experimental.pallas import tpu as pltpu
from jax.sharding import PartitionSpec as P

HEAD_DIM = 128


ROPE_BASE = 500000.0
EPS = 1e-05
NEG_FILL = -1e30


def rope_tables(rel_pos, head_dim):
    half_dim = head_dim // 2
    freq_index = jnp.arange(half_dim, dtype=jnp.float32)
    inv_freq = jnp.exp(freq_index * (-2.0 * math.log(ROPE_BASE) / head_dim))
    angles = rel_pos.astype(jnp.float32)[:, None] * inv_freq[None, :]
    return (jnp.cos(angles), jnp.sin(angles))


def rotate(field, cosine, sine_val, num_heads, head_dim):
    row_count = field.shape[0]
    half_dim = head_dim // 2
    shaped = field.astype(jnp.float32).reshape(row_count, num_heads, head_dim)
    first_half = shaped[..., :half_dim]
    second_half = shaped[..., half_dim:]
    cos_b = cosine[:, None, :]
    sin_b = sine_val[:, None, :]
    turned = jnp.concatenate(
        [first_half * cos_b - second_half * sin_b, second_half * cos_b + first_half * sin_b],
        axis=-1,
    )
    return turned.reshape(row_count, num_heads * head_dim).astype(jnp.bfloat16)


def doc_starts(doc_lengths, positions):
    doc_ends = jnp.cumsum(doc_lengths)
    starts = doc_ends - doc_lengths
    inside = starts[None, :] <= positions[:, None]
    return jnp.max(jnp.where(inside, starts[None, :], 0), axis=1)


MESH = pl.DeviceIdType.MESH


def dp_neighbours():
    dp_at = lax.axis_index("dp")
    ctx_at = lax.axis_index("ctx")
    ring = (dp_at // 4) * 4
    x_at = dp_at % 4
    right = (ring + (x_at + 1) % 4, ctx_at)
    left = (ring + (x_at + 3) % 4, ctx_at)
    across = ((dp_at + 4) % 8, ctx_at)
    return right, left, across


BLOCKS = ((0, 0), (1, 0), (0, 1), (0, 3), (0, 2), (1, 1), (1, 2), (1, 3))
SLOT = {name: at for at, name in enumerate(BLOCKS)}


def mlp_kernel(
    normed_ref, resid_ref, gate_hbm, up_hbm, down_hbm, out_ref,
    tokens, gate_w, up_w, down_w, hidden, sums,
    far_1, far_2, near_1, near_2, cross_1, cross_2,
    local_sem, send_sem, recv_sem,
):
    right, left, across = dp_neighbours()
    rows = tokens.shape[1]
    q = rows // 4
    low, high = pl.ds(0, 2 * q), pl.ds(2 * q, 2 * q)
    part = [pl.ds(i * q, q) for i in range(4)]

    own = pltpu.make_async_copy(normed_ref, tokens.at[0], local_sem.at[0])
    own.start()
    loads = [
        pltpu.make_async_copy(gate_hbm, gate_w, local_sem.at[1]),
        pltpu.make_async_copy(up_hbm, up_w, local_sem.at[2]),
        pltpu.make_async_copy(down_hbm, down_w, local_sem.at[3]),
    ]

    barrier = pltpu.get_barrier_semaphore()
    for peer in (right, left, across):
        pl.semaphore_signal(barrier, inc=1, device_id=peer, device_id_type=MESH)
    pl.semaphore_wait(barrier, 3)

    def slot(dz, dx):
        return SLOT[(dz, dx)]

    plan = {}

    def add(name, src, dst, peer):
        plan[name] = (src, dst, peer, len(plan))

    def copy(name):
        src, dst, peer, at = plan[name]
        return pltpu.make_async_remote_copy(
            src_ref=src, dst_ref=dst, send_sem=send_sem.at[at], recv_sem=recv_sem.at[at],
            device_id=peer, device_id_type=MESH,
        )

    def tok(dz, dx, sel):
        return tokens.at[slot(dz, dx), sel]

    def res(dz, dx, sel):
        return sums.at[slot(dz, dx), sel]

    for i in range(4):
        add(("r", 0, i), tok(0, 0, part[i]), tok(0, 3, part[i]), right)
        add(("l", 0, i), tok(0, 0, part[i]), tok(0, 1, part[i]), left)
    for i in range(2):
        add(("r", 1, i), tok(1, 0, part[i]), tok(1, 3, part[i]), right)
        add(("l", 1, i), tok(1, 0, part[i]), tok(1, 1, part[i]), left)
    for dz, i in ((0, 0), (0, 2), (1, 0)):
        add(("rr", dz, i), tok(dz, 3, part[i]), tok(dz, 2, part[i]), right)
        add(("ll", dz, i + 1), tok(dz, 1, part[i + 1]), tok(dz, 2, part[i + 1]), left)
    add(("z", 0, 0), tok(0, 0, low), tok(1, 0, low), across)
    for dx in range(4):
        add(("z", dx, 1), tok(0, dx, high), tok(1, dx, high), across)
    for dz in range(2):
        add(("fr", dz), res(dz, 2, part[0]), far_1.at[dz, 0], right)
        add(("fl", dz), res(dz, 2, part[1]), far_1.at[dz, 1], left)
        add(("nr", dz), res(dz, 1, low), near_1.at[dz, 0], right)
        add(("nl", dz), res(dz, 3, low), near_1.at[dz, 1], left)
    add("fr2", res(0, 2, part[2]), far_2.at[0], right)
    add("fl2", res(0, 2, part[3]), far_2.at[1], left)
    add("nr2", res(0, 1, high), near_2.at[0], right)
    add("nl2", res(0, 3, high), near_2.at[1], left)
    for dx in range(4):
        add(("sz", dx), res(1, dx, high), cross_2.at[dx], across)
    add("sz1", res(1, 0, low), cross_1, across)

    def start(*names):
        for name in names:
            copy(name).start()

    def arrived(*names):
        for name in names:
            copy(name).wait_recv()

    def grow(dz, dx, sel, *terms):
        ref = res(dz, dx, sel)
        total = ref[...].astype(jnp.float32)
        for term in terms:
            total = total + term[...].astype(jnp.float32)
        ref[...] = total.astype(jnp.bfloat16)

    own.wait()
    start(("z", 0, 0), ("r", 0, 2), ("l", 0, 3), ("r", 0, 3), ("l", 0, 2), ("z", 0, 1))
    start(("r", 0, 0), ("l", 0, 1), ("r", 0, 1), ("l", 0, 0))
    for load in loads:
        load.start()

    def step(at, carry):
        @pl.when(at == 0)
        def _():
            for load in loads:
                load.wait()

        @pl.when(at == 1)
        def _():
            arrived(("r", 0, 2))
            start(("rr", 0, 2))
            arrived(("l", 0, 3))
            start(("ll", 0, 3))
            arrived(("l", 0, 2))
            start(("z", 1, 1))
            arrived(("r", 0, 0))
            start(("rr", 0, 0))
            arrived(("l", 0, 1))
            start(("ll", 0, 1))
            arrived(("z", 0, 0))
            start(("r", 1, 0), ("l", 1, 1), ("r", 1, 1), ("l", 1, 0))
            arrived(("z", 0, 1))

        @pl.when(at == 2)
        def _():
            arrived(("rr", 0, 2), ("ll", 0, 3))
            start(("z", 2, 1))
            arrived(("r", 0, 3))
            start(("z", 3, 1))
            arrived(("l", 0, 0))

        @pl.when(at == 3)
        def _():
            arrived(("r", 0, 1))

        @pl.when(at == 4)
        def _():
            arrived(("r", 1, 0))
            start(("rr", 1, 0))
            arrived(("l", 1, 1))
            start(("ll", 1, 1))
            arrived(("rr", 0, 0), ("ll", 0, 1))

        @pl.when(at == 5)
        def _():
            arrived(("l", 1, 0), ("z", 1, 1))

        @pl.when(at == 6)
        def _():
            arrived(("rr", 1, 0), ("ll", 1, 1), ("z", 2, 1))

        @pl.when(at == 7)
        def _():
            arrived(("r", 1, 1), ("z", 3, 1))

        block = tokens[at]
        width = gate_w.shape[1]
        for col in range(0, width, 256):
            cols = slice(col, min(col + 256, width))
            gate_val = jnp.dot(block, gate_w[:, cols], preferred_element_type=jnp.float32)
            up_val = jnp.dot(block, up_w[:, cols], preferred_element_type=jnp.float32)
            act = gate_val / (1.0 + jnp.exp(-gate_val)) * up_val
            hidden[:, cols] = act.astype(jnp.bfloat16)
        held = hidden[...]
        for col in range(0, down_w.shape[1], 512):
            cols = slice(col, col + 512)
            piece = jnp.dot(held, down_w[:, cols], preferred_element_type=jnp.float32)
            sums[at, :, cols] = piece.astype(jnp.bfloat16)

        @pl.when(at == 4)
        def _():
            start(("fr", 0), ("fl", 0))

        @pl.when(at == 6)
        def _():
            start(("fr", 1), ("fl", 1), ("sz", 2), ("sz", 1))

        @pl.when(at == 7)
        def _():
            start(("sz", 3), ("sz", 0))

        return carry

    lax.fori_loop(0, 8, step, 0)

    for dz in range(2):
        arrived(("fr", dz))
        grow(dz, 1, part[0], far_1.at[dz, 0])
        start(("nr", dz))
        arrived(("fl", dz))
        grow(dz, 3, part[1], far_1.at[dz, 1])
        start(("nl", dz))
    arrived(("sz", 2))
    grow(0, 2, high, cross_2.at[2])
    start("fr2", "fl2")
    arrived(("sz", 1))
    grow(0, 1, high, cross_2.at[1])
    arrived(("nr", 0), ("nl", 0))
    grow(0, 0, low, near_1.at[0, 0], near_1.at[0, 1])
    arrived(("nr", 1), ("nl", 1))
    grow(1, 0, low, near_1.at[1, 0], near_1.at[1, 1])
    start("sz1")
    arrived("fr2")
    grow(0, 1, part[2], far_2.at[0])
    start("nr2")
    arrived(("sz", 3), "fl2")
    grow(0, 3, high, cross_2.at[3])
    grow(0, 3, part[3], far_2.at[1])
    start("nl2")

    def finish(sel, *terms):
        total = res(0, 0, sel)[...].astype(jnp.float32)
        for term in terms:
            total = total + term[...].astype(jnp.float32)
        out_ref[sel, :] = (resid_ref[sel, :] + total).astype(jnp.bfloat16)

    arrived(("sz", 0), "nr2", "nl2")
    finish(high, cross_2.at[0], near_2.at[0], near_2.at[1])
    arrived("sz1")
    finish(low, cross_1)
    for name in plan:
        copy(name).wait_send()


def mlp_phase(normed, residual_sum, w_gate, w_up, w_down):
    rows, width = normed.shape
    half, quarter = rows // 2, rows // 4
    ff = w_gate.shape[1]
    anywhere = pl.BlockSpec(memory_space=pl.ANY)
    vmem = pl.BlockSpec(memory_space=pltpu.VMEM)
    bf16 = jnp.bfloat16
    copies = 8 + 4 + 6 + 5 + 8 + 4 + 5
    return pl.pallas_call(
        mlp_kernel,
        out_shape=jax.ShapeDtypeStruct((rows, width), bf16),
        in_specs=[anywhere, vmem, anywhere, anywhere, anywhere],
        out_specs=vmem,
        scratch_shapes=[
            pltpu.VMEM((8, rows, width), bf16),
            pltpu.VMEM((width, ff), bf16),
            pltpu.VMEM((width, ff), bf16),
            pltpu.VMEM((ff, width), bf16),
            pltpu.VMEM((rows, ff), bf16),
            pltpu.VMEM((8, rows, width), bf16),
            pltpu.VMEM((2, 2, quarter, width), bf16),
            pltpu.VMEM((2, quarter, width), bf16),
            pltpu.VMEM((2, 2, half, width), bf16),
            pltpu.VMEM((2, half, width), bf16),
            pltpu.VMEM((half, width), bf16),
            pltpu.VMEM((4, half, width), bf16),
            pltpu.SemaphoreType.DMA((4,)),
            pltpu.SemaphoreType.DMA((copies,)),
            pltpu.SemaphoreType.DMA((copies,)),
        ],
        compiler_params=pltpu.CompilerParams(
            collective_id=1, has_side_effects=True, vmem_limit_bytes=67043328
        ),
        name="mlp_exchange",
    )(normed, residual_sum, w_gate, w_up, w_down)


REACH = 16


def attention_kernel(
    q_ref, k_ref, v_ref, start_ref, out_ref,
    slots, q_rows, row_max, sums, weighted, send_sem, recv_sem,
):
    ctx_count = lax.axis_size("ctx")
    total = lax.axis_size("dp") * ctx_count
    me = lax.axis_index("dp") * ctx_count + lax.axis_index("ctx")
    ahead = (me + 1) % total
    behind = (me + total - 1) % total
    rows = k_ref.shape[0]
    kv_heads, group_rows, head_dim = q_rows.shape
    group = group_rows // rows
    scale = 1.0 / math.sqrt(head_dim)
    barrier = pltpu.get_barrier_semaphore()
    pl.semaphore_signal(
        barrier, inc=1, device_id=(behind // ctx_count, behind % ctx_count), device_id_type=MESH
    )
    slots[0, 0] = k_ref[...]
    slots[0, 1] = v_ref[...]
    received = jnp.minimum(me, REACH)
    sent = jnp.where(me == total - 1, 0, jnp.minimum(me + 1, REACH))

    def onward(t):
        return pltpu.make_async_remote_copy(
            src_ref=slots.at[t], dst_ref=slots.at[t + 1],
            send_sem=send_sem.at[t], recv_sem=recv_sem.at[t],
            device_id=(ahead // ctx_count, ahead % ctx_count), device_id_type=MESH,
        )

    pl.semaphore_wait(barrier, 1)

    @pl.when(sent > 0)
    def _():
        onward(0).start()

    for h in range(kv_heads):
        for g in range(group):
            at = (h * group + g) * head_dim
            q_rows[h, g * rows:(g + 1) * rows, :] = q_ref[:, at:at + head_dim]
    row_max[...] = jnp.full(row_max.shape, NEG_FILL, jnp.float32)
    sums[...] = jnp.zeros(sums.shape, jnp.float32)
    weighted[...] = jnp.zeros(weighted.shape, jnp.float32)

    def step(t, carry):
        @pl.when(t > 0)
        def _():
            onward(t - 1).wait_recv()

        @pl.when((t > 0) & (t < sent))
        def _():
            onward(t).start()

        key_at = (me - t) * rows + lax.broadcasted_iota(jnp.int32, (rows, rows), 1)
        query_at = me * rows + lax.broadcasted_iota(jnp.int32, (rows, rows), 0)
        allowed = (key_at >= start_ref[...]) & (key_at <= query_at)
        for h in range(kv_heads):
            cols = slice(h * head_dim, (h + 1) * head_dim)
            scores = lax.dot_general(
                q_rows[h], slots[t, 0, :, cols], (((1,), (1,)), ((), ())),
                preferred_element_type=jnp.float32,
            )
            scores = jnp.where(
                allowed[None], (scores * scale).reshape(group, rows, rows), NEG_FILL
            ).reshape(group_rows, rows)
            old_max = row_max[h]
            new_max = jnp.maximum(old_max, jnp.max(scores, axis=-1, keepdims=True))
            weights = jnp.exp(scores - new_max)
            factor = jnp.exp(old_max - new_max)
            row_max[h] = new_max
            sums[h] = sums[h] * factor + weights
            weighted[h] = weighted[h] * factor + jnp.dot(
                weights.astype(jnp.bfloat16), slots[t, 1, :, cols],
                preferred_element_type=jnp.float32,
            )
        return carry

    lax.fori_loop(0, received + 1, step, 0)
    for h in range(kv_heads):
        head_rows = weighted[h] / jnp.sum(sums[h], axis=-1, keepdims=True)
        for g in range(group):
            at = (h * group + g) * head_dim
            out_ref[:, at:at + head_dim] = head_rows[g * rows:(g + 1) * rows].astype(jnp.bfloat16)

    def drain(t, carry):
        onward(t).wait_send()
        return carry

    lax.fori_loop(0, sent, drain, 0)


def attention_phase(q_rot, k_rot, values, query_start):
    rows, width = q_rot.shape
    kv_width = k_rot.shape[1]
    kv_heads = kv_width // HEAD_DIM
    group_rows = width // kv_width * rows
    vmem = pl.BlockSpec(memory_space=pltpu.VMEM)
    per_row = (kv_heads, group_rows, HEAD_DIM)
    starts = jnp.broadcast_to(query_start[:, None], (rows, rows))
    return pl.pallas_call(
        attention_kernel,
        out_shape=jax.ShapeDtypeStruct((rows, width), jnp.bfloat16),
        in_specs=[vmem, vmem, vmem, vmem],
        out_specs=vmem,
        scratch_shapes=[
            pltpu.VMEM((REACH + 1, 2, rows, kv_width), jnp.bfloat16),
            pltpu.VMEM(per_row, jnp.bfloat16),
            pltpu.VMEM(per_row, jnp.float32),
            pltpu.VMEM(per_row, jnp.float32),
            pltpu.VMEM(per_row, jnp.float32),
            pltpu.SemaphoreType.DMA((REACH,)),
            pltpu.SemaphoreType.DMA((REACH,)),
        ],
        compiler_params=pltpu.CompilerParams(
            collective_id=2, has_side_effects=True, vmem_limit_bytes=33554432
        ),
        name="attention_chain",
    )(q_rot, k_rot, values, starts)


def per_device(resid, query, keys, values, doc_lengths, w_out, norm_gain, w_gate, w_up, w_down):
    tok_rows = resid.shape[0]
    head_dim = HEAD_DIM
    kv_heads = keys.shape[1] // head_dim
    num_heads = query.shape[1] // head_dim
    my_block = lax.axis_index(("dp", "ctx"))
    local_index = jnp.arange(tok_rows, dtype=jnp.int32)
    query_pos = my_block * tok_rows + local_index
    query_start = doc_starts(doc_lengths, query_pos)
    cosine, sine_val = rope_tables(query_pos - query_start, head_dim)
    q_rot = rotate(query, cosine, sine_val, num_heads, head_dim)
    k_rot = rotate(keys, cosine, sine_val, kv_heads, head_dim)
    heads_out = attention_phase(q_rot, k_rot, values, query_start)
    spread = lax.all_to_all(heads_out, "dp", split_axis=1, concat_axis=0, tiled=True)
    partial = jnp.dot(spread, w_out, preferred_element_type=jnp.float32).astype(jnp.bfloat16)
    parts = lax.all_to_all(partial, "dp", split_axis=0, concat_axis=0, tiled=True)
    projected = jnp.sum(parts.reshape(-1, tok_rows, parts.shape[1]).astype(jnp.float32), axis=0)
    residual_sum = resid.astype(jnp.float32) + projected
    mean_sq = jnp.mean(residual_sum * residual_sum, axis=1, keepdims=True)
    normed = (residual_sum * lax.rsqrt(mean_sq + EPS) * norm_gain).astype(jnp.bfloat16)
    return mlp_phase(normed, residual_sum, w_gate, w_up, w_down)


def solution(mesh):
    return jax.shard_map(
        per_device,
        mesh=mesh,
        in_specs=(
            P(("dp", "ctx"), None),
            P(("dp", "ctx"), None),
            P(("dp", "ctx"), None),
            P(("dp", "ctx"), None),
            P(),
            P("dp", None),
            P(),
            P(None, "dp"),
            P(None, "dp"),
            P("dp", None),
        ),
        out_specs=P(("dp", "ctx"), None),
        check_vma=False,
    )
```
